32 devices in a mesh: seq: 4 (over z), grp: 8 (over y, x, core).
Axes of the slice: x: 2, y: 2, z: 4, core: 2. Of those that a mesh axis runs over, the one named last changes fastest.
Arguments:
- self_query: bfloat16 [8, 512, 5120], P('grp', 'seq'), may hold values from -250 to 250
- self_key: bfloat16 [8, 512, 5120], P('grp', 'seq'), may hold values from -12 to 12
- self_value: bfloat16 [8, 512, 5120], P('grp', 'seq'), may hold values from -6 to 6
- self_upstream: bfloat16 [8, 512, 5120], P('grp', 'seq'), may hold values from -6 to 6
- cross_query: bfloat16 [8, 512, 5120], P('grp', 'seq'), may hold values from -250 to 250
- context_key: bfloat16 [512, 5120], replicated, may hold values from -12 to 12
- context_value: bfloat16 [512, 5120], replicated, may hold values from -6 to 6
- cross_upstream: bfloat16 [8, 512, 5120], P('grp', 'seq'), may hold values from -6 to 6
Outputs:
- query_grad: bfloat16 [8, 512, 5120], P('grp', 'seq')
- key_grad: bfloat16 [8, 512, 5120], P('grp', 'seq')
- value_grad: bfloat16 [8, 512, 5120], P('grp', 'seq')
- cross_query_grad: bfloat16 [8, 512, 5120], P('grp', 'seq')
- context_key_grad: float32 [512, 5120], P(None, 'seq')
- context_value_grad: float32 [512, 5120], P(None, 'seq')
The draws below stay inside these ranges and needn't reach their ends.
All inputs are finite; a program needn't handle non-finite values.
Results may differ from the reference program's by a relative error of at most 0.013.
Values may be sent and summed in bfloat16 or wider, within the bound.
No kernel may reach another device: no remote copies, remote signals or barrier semaphores. Data moves between devices by JAX's collectives and lax.ppermute only.
A program may use at most 256 MiB of HBM per device.

```python
import jax
import jax.numpy as jnp
from jax import lax

D = 5120
HEADS = 40
HD = 128
CTX = 512
LEN = 512
SAMPLES = 8


def drawn_pair(key, salt, key_samples, key_count):
    base = jax.random.fold_in(key, salt)
    query_key, keys_key = jax.random.split(base, 2)
    queries = jax.random.truncated_normal(query_key, -6.0, 6.0, (SAMPLES, LEN, HEADS, HD), jnp.float32)
    keyset = jax.random.truncated_normal(keys_key, -6.0, 6.0, (key_samples, key_count, HEADS, HD), jnp.float32)
    return (queries.reshape(SAMPLES, LEN, HEADS * HD), keyset.reshape(key_samples, key_count, HEADS * HD))


def draw_self_query(key, part):
    return drawn_pair(key, 11, SAMPLES, LEN)[0].astype(jnp.bfloat16)


def draw_self_key(key, part):
    return drawn_pair(key, 11, SAMPLES, LEN)[1].astype(jnp.bfloat16)


def draw_cross_query(key, part):
    return drawn_pair(key, 23, 1, CTX)[0].astype(jnp.bfloat16)


def draw_context_key(key, part):
    return drawn_pair(key, 23, 1, CTX)[1][0].astype(jnp.bfloat16)


def raised(values, own_key, source, target, parts, factor):
    owner, partner = [(jnp.arange(values.shape[position]) // (values.shape[position] // parts)).reshape([-1 if axis == position else 1 for axis in range(values.ndim)]) for position in (source, target)]
    chosen = jax.random.permutation(own_key, parts)[partner]
    strong = (owner == chosen) | (owner == (partner + parts // 2) % parts)
    return jnp.where(strong, factor * values, values)


def level_of(rng, shape, cuts, low, top_value):
    def one(axis_at, shards_of):
        draws = jax.random.uniform(jax.random.fold_in(jax.random.fold_in(rng, 6), axis_at), (shards_of,), jnp.float32, low / len(cuts), top_value / len(cuts))
        return jnp.repeat(jnp.exp(draws), shape[axis_at] // shards_of).reshape((-1,) + (1,) * (len(shape) - axis_at - 1))

    loudness = one(*cuts[0])
    for cut in cuts[1:]:
        loudness = loudness * one(*cut)
    return loudness


def noise(own_key, shape, spread, bound, cuts=(), kind=jnp.bfloat16):
    level = level_of(own_key, shape, cuts, -0.22, 0.18) if cuts else 1.0
    values = jax.random.normal(own_key, shape, jnp.float32) * spread * level
    return jnp.minimum(jnp.maximum(values, -bound), bound).astype(kind)


def noise_with(rng, shape, width, limit, cuts, heavy, dtype=jnp.bfloat16):
    result = width * jax.random.normal(rng, shape, jnp.float32)
    if cuts:
        result = result * level_of(rng, shape, cuts, -0.22, 0.18)
    return jnp.clip(raised(result, jax.random.fold_in(rng, 3), *heavy), -limit, limit).astype(dtype)


def setup_inputs(seed: int = 0) -> dict:
    splits = jax.random.split(jax.random.key(seed), 9)
    return {
        "self_query": draw_self_query(jax.random.fold_in(splits[8], 71), 0),
        "self_key": draw_self_key(jax.random.fold_in(splits[8], 71), 0),
        "self_value": noise(splits[2], (SAMPLES, LEN, D), 1.0, 6.0, ((0, 8), (1, 4))),
        "self_upstream": noise(splits[3], (SAMPLES, LEN, D), 1.0, 6.0, ((0, 8), (1, 4))),
        "cross_query": draw_cross_query(jax.random.fold_in(splits[8], 71), 0),
        "context_key": draw_context_key(jax.random.fold_in(splits[8], 71), 0),
        "context_value": noise(splits[6], (CTX, D), 1.0, 6.0),
        "cross_upstream": noise_with(splits[7], (SAMPLES, LEN, D), 1.0, 6.0, ((0, 8), (1, 4)), (1, 2, 4, 2.0)),
    }


def attend_back(queries, key_in, value_in, upstream):
    scaling = HD ** -0.5
    query_f = queries.astype(jnp.float32)
    key_f = key_in.astype(jnp.float32)
    value_f = value_in.astype(jnp.float32)
    upstream_f = upstream.astype(jnp.float32)
    scores = jnp.einsum("nhe,mhe->hnm", query_f, key_f) * scaling
    weights = jax.nn.softmax(scores, axis=-1)
    rounded = lax.optimization_barrier(weights.astype(jnp.bfloat16)).astype(jnp.float32)
    output = jnp.einsum("hnm,mhe->nhe", rounded, value_f)
    row_inner = jnp.sum(upstream_f * output, axis=-1)
    grad_prob = jnp.einsum("nhe,mhe->hnm", upstream_f, value_f)
    grad_score = weights * (grad_prob - jnp.transpose(row_inner)[:, :, None]) * scaling
    grad_score = lax.optimization_barrier(grad_score.astype(jnp.bfloat16)).astype(jnp.float32)
    query_grad = jnp.einsum("hnm,mhe->nhe", grad_score, key_f)
    key_grad = jnp.einsum("hnm,nhe->mhe", grad_score, query_f)
    value_grad = jnp.einsum("hnm,nhe->mhe", rounded, upstream_f)
    return query_grad, key_grad, value_grad


def reference(self_query, self_key, self_value, self_upstream, cross_query, context_key, context_value, cross_upstream):
    layout = (SAMPLES, LEN, HEADS, HD)

    def one_sample(pieces):
        grads = attend_back(pieces[0], pieces[1], pieces[2], pieces[3])
        return (grads[0].astype(jnp.bfloat16).reshape(LEN, D),
                grads[1].astype(jnp.bfloat16).reshape(LEN, D),
                grads[2].astype(jnp.bfloat16).reshape(LEN, D))

    query_grad, key_grad, value_grad = lax.map(
        one_sample,
        (self_query.reshape(layout), self_key.reshape(layout), self_value.reshape(layout), self_upstream.reshape(layout)))
    context_heads = context_key.reshape(CTX, HEADS, HD)
    value_heads = context_value.reshape(CTX, HEADS, HD)

    def cross_step(totals, pieces):
        grads = attend_back(pieces[0], context_heads, value_heads, pieces[1])
        return (totals[0] + grads[1], totals[1] + grads[2]), grads[0].astype(jnp.bfloat16).reshape(LEN, D)

    zero_sum = jnp.zeros((CTX, HEADS, HD), jnp.float32)
    totals, cross_grad = lax.scan(cross_step, (zero_sum, zero_sum),
                                  (cross_query.reshape(layout), cross_upstream.reshape(layout)))
    return (query_grad, key_grad, value_grad, cross_grad,
            totals[0].reshape(CTX, D), totals[1].reshape(CTX, D))
```

```python
import math

import jax
import jax.numpy as jnp
from jax import lax
from jax.experimental import pallas as pl
from jax.experimental.pallas import tpu as pltpu
from jax.sharding import PartitionSpec as P


HD = 128
SCALE = HD ** (-0.5)
LOG2E = math.log2(math.e)
PIECES = 2
F32 = jnp.float32
BF16 = jnp.bfloat16
ANY = pl.BlockSpec(memory_space=pl.ANY)
VMEM_LIMIT = 56 * 1024 * 1024


def columns_of(partner, width, first):
    owner = lax.axis_index("seq") ^ partner
    return pl.multiple_of(owner * width + first, HD)


def pack(arrays, count, width, first, piece):
    rows = arrays[0].shape[0]
    kinds = len(arrays)
    order = [j for j in range(count - 1, 0, -1)] + [0]

    def body(*refs):
        ins = refs[:kinds]
        outs = refs[kinds : kinds + count]
        held, got, sent = refs[kinds + count :]

        def fetch(j, a):
            return pltpu.make_async_copy(
                ins[a].at[:, pl.ds(columns_of(j, width, first), piece)], held.at[j, a], got.at[j, a]
            )

        def store(j):
            return pltpu.make_async_copy(held.at[j], outs[j], sent.at[j])

        for j in order:
            for a in range(kinds):
                fetch(j, a).start()
        for j in order:
            for a in range(kinds):
                fetch(j, a).wait()
            store(j).start()
        for j in order:
            store(j).wait()

    size = kinds * rows * piece * 2 * count
    return pl.pallas_call(
        body,
        out_shape=[jax.ShapeDtypeStruct((kinds, rows, piece), BF16)] * count,
        in_specs=[ANY] * kinds,
        out_specs=[ANY] * count,
        scratch_shapes=[
            pltpu.VMEM((count, kinds, rows, piece), BF16),
            pltpu.SemaphoreType.DMA((count, kinds)),
            pltpu.SemaphoreType.DMA((count,)),
        ],
        compiler_params=pltpu.CompilerParams(vmem_limit_bytes=VMEM_LIMIT),
        cost_estimate=pl.CostEstimate(flops=0, transcendentals=0, bytes_accessed=2 * size),
        name="pack",
    )(*arrays)


def unpack(pieces, before, full, width, first):
    count = len(pieces)
    kinds, rows, piece = pieces[0].shape
    held_count = len(before)

    def body(*refs):
        ins = refs[:count]
        outs = refs[count + held_count : count + held_count + kinds]
        held, got, sent = refs[count + held_count + kinds :]

        def fetch(j):
            return pltpu.make_async_copy(ins[j], held.at[j], got.at[j])

        def store(j, a):
            return pltpu.make_async_copy(
                held.at[j, a], outs[a].at[:, pl.ds(columns_of(j, width, first), piece)], sent.at[j, a]
            )

        for j in range(count):
            fetch(j).start()
        for j in range(count):
            fetch(j).wait()
            for a in range(kinds):
                store(j, a).start()
        for j in range(count):
            for a in range(kinds):
                store(j, a).wait()

    size = kinds * rows * piece * 2 * count
    return pl.pallas_call(
        body,
        out_shape=[jax.ShapeDtypeStruct((rows, full), BF16)] * kinds,
        in_specs=[ANY] * (count + held_count),
        out_specs=[ANY] * kinds,
        scratch_shapes=[
            pltpu.VMEM((count, kinds, rows, piece), BF16),
            pltpu.SemaphoreType.DMA((count,)),
            pltpu.SemaphoreType.DMA((count, kinds)),
        ],
        input_output_aliases={count + a: a for a in range(held_count)},
        compiler_params=pltpu.CompilerParams(vmem_limit_bytes=VMEM_LIMIT),
        cost_estimate=pl.CostEstimate(flops=0, transcendentals=0, bytes_accessed=2 * size),
        name="unpack",
    )(*pieces, *before)


def dot(a, b, over_a, over_b):
    return lax.dot_general(a, b, (((over_a,), (over_b,)), ((), ())), preferred_element_type=F32)


def back(queries, keys, values, upstream):
    scores = dot(keys, queries, 1, 1)
    top = jnp.max(scores, axis=0, keepdims=True)
    raw = jnp.exp2((scores - top) * (SCALE * LOG2E))
    weights = raw * (1.0 / jnp.sum(raw, axis=0, keepdims=True))
    grad_prob = dot(values, upstream, 1, 1)
    rounded = weights.astype(BF16)
    delta = jnp.sum(rounded.astype(F32) * grad_prob, axis=0, keepdims=True)
    grad_score = (weights * (grad_prob - delta) * SCALE).astype(BF16)
    value_grad = dot(rounded, upstream, 1, 0)
    key_grad = dot(grad_score, queries, 1, 0)
    query_grad = dot(grad_score, keys, 0, 0)
    return query_grad, key_grad, value_grad


def self_back(pieces):
    count = len(pieces)
    kinds, rows, piece = pieces[0].shape
    heads = piece // HD

    def body(*refs):
        ins, outs = refs[:count], refs[count:]
        joined = [jnp.concatenate([ref[a] for ref in ins], axis=0) for a in range(kinds)]
        grads = back(*joined)
        for a in range(3):
            value = grads[a].astype(BF16)
            for j in range(count):
                outs[j][a] = value[j * rows : (j + 1) * rows]

    tokens = count * rows
    return pl.pallas_call(
        body,
        grid=(heads,),
        out_shape=[jax.ShapeDtypeStruct((3, rows, piece), BF16)] * count,
        in_specs=[pl.BlockSpec((kinds, rows, HD), lambda h: (0, 0, h))] * count,
        out_specs=[pl.BlockSpec((3, rows, HD), lambda h: (0, 0, h))] * count,
        compiler_params=pltpu.CompilerParams(
            vmem_limit_bytes=VMEM_LIMIT, dimension_semantics=("arbitrary",)
        ),
        cost_estimate=pl.CostEstimate(
            flops=10 * tokens * tokens * piece,
            transcendentals=tokens * tokens * heads,
            bytes_accessed=7 * tokens * piece * 2,
        ),
        name="self_back",
    )(*pieces)


def cross_back(queries, keys, values, upstream, core):
    rows, full = queries.shape
    text = keys.shape[0]
    heads = full // HD
    group = 2 if heads % 2 == 0 else 1
    wide = group * HD

    def body(core_ref, q_ref, k_ref, v_ref, g_ref, dq_ref, own_ref, other_ref):
        for i in range(group):
            at = slice(i * HD, (i + 1) * HD)
            query_grad, key_grad, value_grad = back(q_ref[:, at], k_ref[:, at], v_ref[:, at], g_ref[:, at])
            dq_ref[:, at] = query_grad.astype(BF16)

            @pl.when(core_ref[0] == 0)
            def _():
                own_ref[:, at] = key_grad.astype(BF16)
                other_ref[:, at] = value_grad.astype(BF16)

            @pl.when(core_ref[0] != 0)
            def _():
                own_ref[:, at] = value_grad.astype(BF16)
                other_ref[:, at] = key_grad.astype(BF16)

    small = pl.BlockSpec((rows, wide), lambda h, c: (0, h))
    large = pl.BlockSpec((text, wide), lambda h, c: (0, h))
    return pl.pallas_call(
        body,
        grid_spec=pltpu.PrefetchScalarGridSpec(
            num_scalar_prefetch=1,
            grid=(heads // group,),
            in_specs=[small, large, large, small],
            out_specs=[small, large, large],
        ),
        out_shape=[
            jax.ShapeDtypeStruct((rows, full), BF16),
            jax.ShapeDtypeStruct((text, full), BF16),
            jax.ShapeDtypeStruct((text, full), BF16),
        ],
        compiler_params=pltpu.CompilerParams(
            vmem_limit_bytes=VMEM_LIMIT, dimension_semantics=("arbitrary",)
        ),
        cost_estimate=pl.CostEstimate(
            flops=10 * rows * text * full,
            transcendentals=rows * text * heads,
            bytes_accessed=2 * full * (3 * rows + 4 * text),
        ),
        name="cross_back",
    )(core, queries, keys, values, upstream)


def swap(value, axis, bit):
    size = lax.axis_size(axis)
    return lax.ppermute(value, axis, [(i, i ^ bit) for i in range(size)])


def side(axis, bit):
    return (lax.axis_index(axis) // bit) % 2


def pick(value, index, dim):
    return lax.dynamic_index_in_dim(value, index, dim, keepdims=False)


def add(a, b):
    return (a.astype(F32) + b.astype(F32)).astype(BF16)


def halve(value, dim, axis, bit):
    mine = side(axis, bit)
    return add(pick(value, mine, dim), swap(pick(value, 1 - mine, dim), axis, bit))


def both(value, other, axis, bit, dim):
    low = side(axis, bit) == 0
    return jnp.stack([jnp.where(low, value, other), jnp.where(low, other, value)], axis=dim)


def reduce_text(own, other):
    grp, seq = lax.axis_size("grp"), lax.axis_size("seq")
    bits = [1 << i for i in range(1, grp.bit_length() - 1)]
    seq_bits = [1 << i for i in range(seq.bit_length() - 1)]
    text, full = own.shape
    total = add(own, swap(other, "grp", 1))
    ways = 2
    split = total.reshape((ways,) + (2,) * len(bits) + (text // (ways * grp // 2), full))
    parts = []
    for way in range(ways):
        part = split[way]
        names = list(bits)
        for bit in bits[way:] + bits[:way]:
            part = halve(part, names.index(bit), "grp", bit)
            names.remove(bit)
        parts.append(part)
    part = jnp.stack(parts)
    part = part.reshape(part.shape[:2] + (2,) * len(seq_bits) + (full // seq,))
    left = list(reversed(seq_bits))
    for bit in seq_bits:
        part = halve(part, 2 + left.index(bit), "seq", bit)
        left.remove(bit)
    for bit in reversed(bits):
        part = both(part, swap(part, "grp", bit), "grp", bit, 1)
    other = swap(part, "grp", 1)
    low = side("grp", 1) == 0
    shape = (text, full // seq)
    return (
        jnp.where(low, part, other).astype(F32).reshape(shape),
        jnp.where(low, other, part).astype(F32).reshape(shape),
    )


def shards(
    self_query,
    self_key,
    self_value,
    self_upstream,
    cross_query,
    context_key,
    context_value,
    cross_upstream,
):
    full = self_query.shape[2]
    seq = lax.axis_size("seq")
    width = full // seq
    heads = width // HD
    cuts = [heads * i // PIECES for i in range(PIECES + 1)]
    spans = [(a * HD, (b - a) * HD) for a, b in zip(cuts, cuts[1:]) if b > a]
    arrays = [self_query[0], self_key[0], self_value[0], self_upstream[0]]

    def exchange(pieces):
        swapped = {j: swap(pieces[j], "seq", j) for j in range(seq - 1, 0, -1)}
        return [pieces[0]] + [swapped[j] for j in range(1, seq)]

    arrived = []
    for first, piece in spans:
        packed = pack(arrays, seq, width, first, piece)
        arrived.append(exchange(packed))
    core = side("grp", 1).astype(jnp.int32).reshape(1)
    cross_grad, own, other = cross_back(
        cross_query[0], context_key, context_value, cross_upstream[0], core
    )
    key_total, value_total = reduce_text(own, other)
    grads = []
    for (first, piece), pieces in zip(spans, arrived):
        parts = self_back(pieces)
        parts = exchange(parts)
        grads = unpack(parts, grads, full, width, first)
    query_grad, key_grad, value_grad = grads
    return query_grad[None], key_grad[None], value_grad[None], cross_grad[None], key_total, value_total


def solution(mesh):
    row = P("grp", "seq", None)
    return jax.shard_map(
        shards,
        mesh=mesh,
        in_specs=(row, row, row, row, row, P(), P(), row),
        out_specs=(row, row, row, row, P(None, "seq"), P(None, "seq")),
        check_vma=False,
    )
```

```python
import math

import jax
import jax.numpy as jnp
from jax import lax
from jax.experimental import pallas as pl
from jax.experimental.pallas import tpu as pltpu
from jax.sharding import PartitionSpec as P


HD = 128
SCALE = HD ** (-0.5)
LOG2E = math.log2(math.e)
PIECES = 2
F32 = jnp.float32
BF16 = jnp.bfloat16
ANY = pl.BlockSpec(memory_space=pl.ANY)
VMEM_LIMIT = 56 * 1024 * 1024


def columns_of(partner, width, first):
    owner = lax.axis_index("seq") ^ partner
    return pl.multiple_of(owner * width + first, HD)


def pack(arrays, count, width, first, piece):
    rows = arrays[0].shape[0]
    kinds = len(arrays)
    order = [j for j in range(count - 1, 0, -1)] + [0]

    def body(*refs):
        ins = refs[:kinds]
        outs = refs[kinds : kinds + count]
        held, got, sent = refs[kinds + count :]

        def fetch(j, a):
            return pltpu.make_async_copy(
                ins[a].at[:, pl.ds(columns_of(j, width, first), piece)], held.at[j, a], got.at[j, a]
            )

        def store(j):
            return pltpu.make_async_copy(held.at[j], outs[j], sent.at[j])

        for j in order:
            for a in range(kinds):
                fetch(j, a).start()
        for j in order:
            for a in range(kinds):
                fetch(j, a).wait()
            store(j).start()
        for j in order:
            store(j).wait()

    size = kinds * rows * piece * 2 * count
    return pl.pallas_call(
        body,
        out_shape=[jax.ShapeDtypeStruct((kinds, rows, piece), BF16)] * count,
        in_specs=[ANY] * kinds,
        out_specs=[ANY] * count,
        scratch_shapes=[
            pltpu.VMEM((count, kinds, rows, piece), BF16),
            pltpu.SemaphoreType.DMA((count, kinds)),
            pltpu.SemaphoreType.DMA((count,)),
        ],
        compiler_params=pltpu.CompilerParams(vmem_limit_bytes=VMEM_LIMIT),
        cost_estimate=pl.CostEstimate(flops=0, transcendentals=0, bytes_accessed=2 * size),
        name="pack",
    )(*arrays)


def unpack(pieces, before, full, width, first):
    count = len(pieces)
    kinds, rows, piece = pieces[0].shape
    held_count = len(before)

    def body(*refs):
        ins = refs[:count]
        outs = refs[count + held_count : count + held_count + kinds]
        held, got, sent = refs[count + held_count + kinds :]

        def fetch(j):
            return pltpu.make_async_copy(ins[j], held.at[j], got.at[j])

        def store(j, a):
            return pltpu.make_async_copy(
                held.at[j, a], outs[a].at[:, pl.ds(columns_of(j, width, first), piece)], sent.at[j, a]
            )

        for j in range(count):
            fetch(j).start()
        for j in range(count):
            fetch(j).wait()
            for a in range(kinds):
                store(j, a).start()
        for j in range(count):
            for a in range(kinds):
                store(j, a).wait()

    size = kinds * rows * piece * 2 * count
    return pl.pallas_call(
        body,
        out_shape=[jax.ShapeDtypeStruct((rows, full), BF16)] * kinds,
        in_specs=[ANY] * (count + held_count),
        out_specs=[ANY] * kinds,
        scratch_shapes=[
            pltpu.VMEM((count, kinds, rows, piece), BF16),
            pltpu.SemaphoreType.DMA((count,)),
            pltpu.SemaphoreType.DMA((count, kinds)),
        ],
        input_output_aliases={count + a: a for a in range(held_count)},
        compiler_params=pltpu.CompilerParams(vmem_limit_bytes=VMEM_LIMIT),
        cost_estimate=pl.CostEstimate(flops=0, transcendentals=0, bytes_accessed=2 * size),
        name="unpack",
    )(*pieces, *before)


def dot(a, b, over_a, over_b):
    return lax.dot_general(a, b, (((over_a,), (over_b,)), ((), ())), preferred_element_type=F32)


def back(queries, keys, values, upstream):
    scores = dot(keys, queries, 1, 1)
    top = jnp.max(scores, axis=0, keepdims=True)
    raw = jnp.exp2((scores - top) * (SCALE * LOG2E))
    weights = raw * (1.0 / jnp.sum(raw, axis=0, keepdims=True))
    grad_prob = dot(values, upstream, 1, 1)
    rounded = weights.astype(BF16)
    delta = jnp.sum(rounded.astype(F32) * grad_prob, axis=0, keepdims=True)
    grad_score = (weights * (grad_prob - delta) * SCALE).astype(BF16)
    value_grad = dot(rounded, upstream, 1, 0)
    key_grad = dot(grad_score, queries, 1, 0)
    query_grad = dot(keys, grad_score, 0, 0).T
    return query_grad, key_grad, value_grad


def self_back(pieces):
    count = len(pieces)
    kinds, rows, piece = pieces[0].shape
    heads = piece // HD

    def body(*refs):
        ins, outs = refs[:count], refs[count:]
        joined = [jnp.concatenate([ref[a] for ref in ins], axis=0) for a in range(kinds)]
        grads = back(*joined)
        for a in range(3):
            value = grads[a].astype(BF16)
            for j in range(count):
                outs[j][a] = value[j * rows : (j + 1) * rows]

    tokens = count * rows
    return pl.pallas_call(
        body,
        grid=(heads,),
        out_shape=[jax.ShapeDtypeStruct((3, rows, piece), BF16)] * count,
        in_specs=[pl.BlockSpec((kinds, rows, HD), lambda h: (0, 0, h))] * count,
        out_specs=[pl.BlockSpec((3, rows, HD), lambda h: (0, 0, h))] * count,
        compiler_params=pltpu.CompilerParams(
            vmem_limit_bytes=VMEM_LIMIT, dimension_semantics=("arbitrary",)
        ),
        cost_estimate=pl.CostEstimate(
            flops=10 * tokens * tokens * piece,
            transcendentals=tokens * tokens * heads,
            bytes_accessed=7 * tokens * piece * 2,
        ),
        name="self_back",
    )(*pieces)


def cross_back(queries, keys, values, upstream, core):
    rows, full = queries.shape
    text = keys.shape[0]
    heads = full // HD
    group = math.gcd(heads, 4)
    wide = group * HD

    def body(core_ref, q_ref, k_ref, v_ref, g_ref, dq_ref, own_ref, other_ref):
        for i in range(group):
            at = slice(i * HD, (i + 1) * HD)
            query_grad, key_grad, value_grad = back(q_ref[:, at], k_ref[:, at], v_ref[:, at], g_ref[:, at])
            dq_ref[:, at] = query_grad.astype(BF16)
            first = core_ref[0] == 0
            own_ref[:, at] = jnp.where(first, key_grad, value_grad).astype(BF16)
            other_ref[:, at] = jnp.where(first, value_grad, key_grad).astype(BF16)

    small = pl.BlockSpec((rows, wide), lambda h, c: (0, h))
    large = pl.BlockSpec((text, wide), lambda h, c: (0, h))
    return pl.pallas_call(
        body,
        grid_spec=pltpu.PrefetchScalarGridSpec(
            num_scalar_prefetch=1,
            grid=(heads // group,),
            in_specs=[small, large, large, small],
            out_specs=[small, large, large],
        ),
        out_shape=[
            jax.ShapeDtypeStruct((rows, full), BF16),
            jax.ShapeDtypeStruct((text, full), BF16),
            jax.ShapeDtypeStruct((text, full), BF16),
        ],
        compiler_params=pltpu.CompilerParams(
            vmem_limit_bytes=VMEM_LIMIT, dimension_semantics=("arbitrary",)
        ),
        cost_estimate=pl.CostEstimate(
            flops=10 * rows * text * full,
            transcendentals=rows * text * heads,
            bytes_accessed=2 * full * (3 * rows + 4 * text),
        ),
        name="cross_back",
    )(core, queries, keys, values, upstream)


def finish(own, other, core):
    rows, full = own.shape
    block = math.gcd(rows, 128)

    def body(core_ref, own_ref, other_ref, key_ref, value_ref):
        first = core_ref[0] == 0
        mine, theirs = own_ref[...].astype(F32), other_ref[...].astype(F32)
        key_ref[...] = jnp.where(first, mine, theirs)
        value_ref[...] = jnp.where(first, theirs, mine)

    spec = pl.BlockSpec((block, full), lambda i, c: (i, 0))
    return pl.pallas_call(
        body,
        grid_spec=pltpu.PrefetchScalarGridSpec(
            num_scalar_prefetch=1, grid=(rows // block,), in_specs=[spec] * 2, out_specs=[spec] * 2
        ),
        out_shape=[jax.ShapeDtypeStruct((rows, full), F32)] * 2,
        compiler_params=pltpu.CompilerParams(dimension_semantics=("arbitrary",)),
        cost_estimate=pl.CostEstimate(flops=0, transcendentals=0, bytes_accessed=12 * rows * full),
        name="finish",
    )(core, own, other)


def swap(value, axis, bit):
    size = lax.axis_size(axis)
    return lax.ppermute(value, axis, [(i, i ^ bit) for i in range(size)])


def side(axis, bit):
    return (lax.axis_index(axis) // bit) % 2


def pick(value, index, dim):
    return lax.dynamic_index_in_dim(value, index, dim, keepdims=False)


def add(a, b):
    return (a.astype(F32) + b.astype(F32)).astype(BF16)


def halve(value, dim, axis, bit):
    mine = side(axis, bit)
    return add(pick(value, mine, dim), swap(pick(value, 1 - mine, dim), axis, bit))


def both(value, other, axis, bit, dim):
    low = side(axis, bit) == 0
    return jnp.stack([jnp.where(low, value, other), jnp.where(low, other, value)], axis=dim)


def reduce_text(own, other, core):
    grp, seq = lax.axis_size("grp"), lax.axis_size("seq")
    bits = [1 << i for i in range(1, grp.bit_length() - 1)]
    seq_bits = [1 << i for i in range(seq.bit_length() - 1)]
    text, full = own.shape
    total = add(own, swap(other, "grp", 1))
    ways = 2
    split = total.reshape((ways,) + (2,) * len(bits) + (text // (ways * grp // 2), full))
    parts = []
    for way in range(ways):
        part = split[way]
        names = list(bits)
        for bit in bits[way:] + bits[:way]:
            part = halve(part, names.index(bit), "grp", bit)
            names.remove(bit)
        parts.append(part)
    part = jnp.stack(parts)
    part = part.reshape(part.shape[:2] + (2,) * len(seq_bits) + (full // seq,))
    left = list(reversed(seq_bits))
    for bit in seq_bits:
        part = halve(part, 2 + left.index(bit), "seq", bit)
        left.remove(bit)
    for bit in reversed(bits):
        part = both(part, swap(part, "grp", bit), "grp", bit, 1)
    shape = (text, full // seq)
    other = swap(part, "grp", 1)
    return finish(part.reshape(shape), other.reshape(shape), core)


def shards(
    self_query,
    self_key,
    self_value,
    self_upstream,
    cross_query,
    context_key,
    context_value,
    cross_upstream,
):
    full = self_query.shape[2]
    seq = lax.axis_size("seq")
    width = full // seq
    heads = width // HD
    cuts = [heads * i // PIECES for i in range(PIECES + 1)]
    spans = [(a * HD, (b - a) * HD) for a, b in zip(cuts, cuts[1:]) if b > a]
    arrays = [self_query[0], self_key[0], self_value[0], self_upstream[0]]

    def exchange(pieces):
        swapped = {j: swap(pieces[j], "seq", j) for j in range(seq - 1, 0, -1)}
        return [pieces[0]] + [swapped[j] for j in range(1, seq)]

    arrived = []
    for first, piece in spans:
        packed = pack(arrays, seq, width, first, piece)
        arrived.append(exchange(packed))
    core = side("grp", 1).astype(jnp.int32).reshape(1)
    cross_grad, own, other = cross_back(
        cross_query[0], context_key, context_value, cross_upstream[0], core
    )
    key_total, value_total = reduce_text(own, other, core)
    grads = []
    for (first, piece), pieces in zip(spans, arrived):
        parts = self_back(pieces)
        parts = exchange(parts)
        grads = unpack(parts, grads, full, width, first)
    query_grad, key_grad, value_grad = grads
    return query_grad[None], key_grad[None], value_grad[None], cross_grad[None], key_total, value_total


def solution(mesh):
    row = P("grp", "seq", None)
    return jax.shard_map(
        shards,
        mesh=mesh,
        in_specs=(row, row, row, row, row, P(), P(), row),
        out_specs=(row, row, row, row, P(None, "seq"), P(None, "seq")),
        check_vma=False,
    )
```

```python
import math

import jax
import jax.numpy as jnp
from jax import lax
from jax.experimental import pallas as pl
from jax.experimental.pallas import tpu as pltpu
from jax.sharding import PartitionSpec as P


HD = 128
SCALE = HD ** (-0.5)
LOG2E = math.log2(math.e)
PIECES = 2
SEQ, GRP = "seq", "grp"
IN_ORDER = "arbitrary"
F32 = jnp.float32
BF16 = jnp.bfloat16
ANY = pl.BlockSpec(memory_space=pl.ANY)
VMEM_LIMIT = 67043328


def columns_of(partner, width, first):
    owner = lax.axis_index(SEQ) ^ partner
    return pl.multiple_of(owner * width + first, HD)


def pack(arrays, count, width, first, piece):
    rows = arrays[0].shape[0]
    kinds = len(arrays)
    order = [j for j in range(count - 1, 0, -1)] + [0]

    def body(*refs):
        ins = refs[:kinds]
        outs = refs[kinds : kinds + count]
        held, got, sent = refs[kinds + count :]

        def fetch(j, a):
            return pltpu.make_async_copy(
                ins[a].at[:, pl.ds(columns_of(j, width, first), piece)], held.at[j, a], got.at[j, a]
            )

        def store(j):
            return pltpu.make_async_copy(held.at[j], outs[j], sent.at[j])

        for j in order:
            for a in range(kinds):
                fetch(j, a).start()
        for j in order:
            for a in range(kinds):
                fetch(j, a).wait()
            store(j).start()
        for j in order:
            store(j).wait()

    size = kinds * rows * piece * 2 * count
    return pl.pallas_call(
        body,
        out_shape=[jax.ShapeDtypeStruct((kinds, rows, piece), BF16)] * count,
        in_specs=[ANY] * kinds,
        out_specs=[ANY] * count,
        scratch_shapes=[
            pltpu.VMEM((count, kinds, rows, piece), BF16),
            pltpu.SemaphoreType.DMA((count, kinds)),
            pltpu.SemaphoreType.DMA((count,)),
        ],
        compiler_params=pltpu.CompilerParams(vmem_limit_bytes=VMEM_LIMIT),
        cost_estimate=pl.CostEstimate(flops=0, transcendentals=0, bytes_accessed=2 * size),
    )(*arrays)


def unpack(pieces, before, full, width, first):
    count = len(pieces)
    kinds, rows, piece = pieces[0].shape
    held_count = len(before)

    def body(*refs):
        ins = refs[:count]
        outs = refs[count + held_count : count + held_count + kinds]
        held, got, sent = refs[count + held_count + kinds :]

        def fetch(j):
            return pltpu.make_async_copy(ins[j], held.at[j], got.at[j])

        def store(j, a):
            return pltpu.make_async_copy(
                held.at[j, a], outs[a].at[:, pl.ds(columns_of(j, width, first), piece)], sent.at[j, a]
            )

        for j in range(count):
            fetch(j).start()
        for j in range(count):
            fetch(j).wait()
            for a in range(kinds):
                store(j, a).start()
        for j in range(count):
            for a in range(kinds):
                store(j, a).wait()

    size = kinds * rows * piece * 2 * count
    return pl.pallas_call(
        body,
        out_shape=[jax.ShapeDtypeStruct((rows, full), BF16)] * kinds,
        in_specs=[ANY] * (count + held_count),
        out_specs=[ANY] * kinds,
        scratch_shapes=[
            pltpu.VMEM((count, kinds, rows, piece), BF16),
            pltpu.SemaphoreType.DMA((count,)),
            pltpu.SemaphoreType.DMA((count, kinds)),
        ],
        input_output_aliases={count + a: a for a in range(held_count)},
        compiler_params=pltpu.CompilerParams(vmem_limit_bytes=VMEM_LIMIT),
        cost_estimate=pl.CostEstimate(flops=0, transcendentals=0, bytes_accessed=2 * size),
    )(*pieces, *before)


def dot(a, b, over_a, over_b):
    return lax.dot_general(a, b, (((over_a,), (over_b,)), ((), ())), preferred_element_type=F32)


def back(queries, keys, values, upstream):
    scores = dot(keys, queries, 1, 1)
    top = jnp.max(scores, axis=0, keepdims=True)
    raw = jnp.exp2((scores - top) * (SCALE * LOG2E))
    weights = raw * (1.0 / jnp.sum(raw, axis=0, keepdims=True))
    grad_prob = dot(values, upstream, 1, 1)
    rounded = weights.astype(BF16)
    delta = jnp.sum(rounded.astype(F32) * grad_prob, axis=0, keepdims=True)
    grad_score = (weights * (grad_prob - delta) * SCALE).astype(BF16)
    value_grad = dot(rounded, upstream, 1, 0)
    key_grad = dot(grad_score, queries, 1, 0)
    query_grad = dot(keys, grad_score, 0, 0).T
    return query_grad, key_grad, value_grad


def self_back(pieces):
    count = len(pieces)
    kinds, rows, piece = pieces[0].shape
    heads = piece // HD
    group = group_of(0, heads) if count * rows <= 512 else 1

    def body(*refs):
        ins, outs = refs[:count], refs[count:]
        for i in range(group):
            at = slice(i * HD, (i + 1) * HD)
            grads = back(*[jnp.concatenate([ref[a, :, at] for ref in ins], axis=0) for a in range(kinds)])
            for a in range(3):
                value = grads[a].astype(BF16)
                for j in range(count):
                    outs[j][a, :, at] = value[j * rows : (j + 1) * rows]

    tokens = count * rows
    return pl.pallas_call(
        body,
        grid=(heads // group,),
        out_shape=[jax.ShapeDtypeStruct((3, rows, piece), BF16)] * count,
        in_specs=[pl.BlockSpec((kinds, rows, group * HD), lambda h: (0, 0, h))] * count,
        out_specs=[pl.BlockSpec((3, rows, group * HD), lambda h: (0, 0, h))] * count,
        compiler_params=pltpu.CompilerParams(
            vmem_limit_bytes=VMEM_LIMIT, dimension_semantics=(IN_ORDER,)
        ),
        cost_estimate=pl.CostEstimate(
            flops=10 * tokens * tokens * piece,
            transcendentals=tokens * tokens * heads,
            bytes_accessed=7 * tokens * piece * 2,
        ),
    )(*pieces)


def cross_back(queries, keys, values, upstream, core, before, first, count):
    rows, full = queries.shape
    text = keys.shape[0]
    group = group_of(first, count)
    wide = group * HD
    start = first // group
    held = len(before)
    width = count * HD

    def body(core_ref, q_ref, k_ref, v_ref, g_ref, *refs):
        dq_ref, own_ref, other_ref = refs[held:]
        for i in range(group):
            at = slice(i * HD, (i + 1) * HD)
            query_grad, key_grad, value_grad = back(q_ref[:, at], k_ref[:, at], v_ref[:, at], g_ref[:, at])
            dq_ref[:, at] = query_grad.astype(BF16)
            low = core_ref[0] == 0
            own_ref[:, at] = jnp.where(low, key_grad, value_grad).astype(BF16)
            other_ref[:, at] = jnp.where(low, value_grad, key_grad).astype(BF16)

    small = pl.BlockSpec((rows, wide), lambda h, c: (0, start + h))
    large = pl.BlockSpec((text, wide), lambda h, c: (0, start + h))
    return pl.pallas_call(
        body,
        grid_spec=pltpu.PrefetchScalarGridSpec(
            num_scalar_prefetch=1,
            grid=(count // group,),
            in_specs=[small, large, large, small] + [ANY] * held,
            out_specs=[small] + [pl.BlockSpec((text, wide), lambda h, c: (0, h))] * 2,
        ),
        out_shape=[
            jax.ShapeDtypeStruct((rows, full), BF16),
            jax.ShapeDtypeStruct((text, width), BF16),
            jax.ShapeDtypeStruct((text, width), BF16),
        ],
        input_output_aliases={5 + i: i for i in range(held)},
        compiler_params=pltpu.CompilerParams(
            vmem_limit_bytes=VMEM_LIMIT, dimension_semantics=(IN_ORDER,)
        ),
        cost_estimate=pl.CostEstimate(
            flops=10 * rows * text * count * HD,
            transcendentals=rows * text * count,
            bytes_accessed=2 * count * HD * (3 * rows + 4 * text),
        ),
    )(core, queries, keys, values, upstream, *before)


def cross_pieces(queries, keys, values, upstream, core, pieces):
    heads = queries.shape[1] // HD
    count = heads // pieces
    grads, sums = [], []
    for i in range(pieces):
        grad, own, other = cross_back(queries, keys, values, upstream, core, grads, i * count, count)
        grads = [grad]
        sums.append((own, other))
    return grads[0], sums


def finish(own, other, core):
    rows, full = own.shape
    block = math.gcd(rows, 128)

    def body(core_ref, own_ref, other_ref, key_ref, value_ref):
        first = core_ref[0] == 0
        mine, theirs = own_ref[...].astype(F32), other_ref[...].astype(F32)
        key_ref[...] = jnp.where(first, mine, theirs)
        value_ref[...] = jnp.where(first, theirs, mine)

    spec = pl.BlockSpec((block, full), lambda i, c: (i, 0))
    return pl.pallas_call(
        body,
        grid_spec=pltpu.PrefetchScalarGridSpec(
            num_scalar_prefetch=1, grid=(rows // block,), in_specs=[spec] * 2, out_specs=[spec] * 2
        ),
        out_shape=[jax.ShapeDtypeStruct((rows, full), F32)] * 2,
        compiler_params=pltpu.CompilerParams(
            vmem_limit_bytes=VMEM_LIMIT, dimension_semantics=(IN_ORDER,)
        ),
        cost_estimate=pl.CostEstimate(flops=0, transcendentals=0, bytes_accessed=12 * rows * full),
    )(core, own, other)


def swap(value, axis, bit):
    size = lax.axis_size(axis)
    return lax.ppermute(value, axis, [(i, i ^ bit) for i in range(size)])


def side(axis, bit):
    return (lax.axis_index(axis) // bit) % 2


def pick(value, index, dim):
    return lax.dynamic_index_in_dim(value, index, dim, keepdims=False)


def add(a, b):
    return (a.astype(F32) + b.astype(F32)).astype(BF16)


def halve(value, dim, axis, bit):
    mine = side(axis, bit)
    return add(pick(value, mine, dim), swap(pick(value, 1 - mine, dim), axis, bit))


def both(value, other, axis, bit, dim):
    low = side(axis, bit) == 0
    return jnp.stack([jnp.where(low, value, other), jnp.where(low, other, value)], axis=dim)


def reduce_text(own, other, core):
    grp, seq = lax.axis_size(GRP), lax.axis_size(SEQ)
    bits = [1 << i for i in range(1, grp.bit_length() - 1)]
    seq_bits = [1 << i for i in range(seq.bit_length() - 1)]
    text, full = own.shape
    total = add(own, swap(other, GRP, 1))
    ways = 2
    split = total.reshape((ways,) + (2,) * len(bits) + (text // (ways * grp // 2), full))
    parts = []
    for way in range(ways):
        part = split[way]
        names = list(bits)
        for bit in bits[way:] + bits[:way]:
            part = halve(part, names.index(bit), GRP, bit)
            names.remove(bit)
        parts.append(part)
    part = jnp.stack(parts)
    part = part.reshape(part.shape[:2] + (2,) * len(seq_bits) + (full // seq,))
    left = list(reversed(seq_bits))
    for bit in seq_bits:
        part = halve(part, 2 + left.index(bit), SEQ, bit)
        left.remove(bit)
    for bit in reversed(bits):
        part = both(part, swap(part, GRP, bit), GRP, bit, 1)
    shape = (text, full // seq)
    return finish(part.reshape(shape), swap(part, GRP, 1).reshape(shape), core)


def split_shards(
    self_query,
    self_key,
    self_value,
    self_upstream,
    cross_query,
    context_key,
    context_value,
    cross_upstream,
):
    full = self_query.shape[2]
    seq = lax.axis_size(SEQ)
    width = full // seq
    heads = width // HD
    cuts = [heads * i // PIECES for i in range(PIECES + 1)]
    spans = [(a * HD, (b - a) * HD) for a, b in zip(cuts, cuts[1:]) if b > a]
    arrays = [self_query[0], self_key[0], self_value[0], self_upstream[0]]

    def exchange(pieces):
        return [pieces[0]] + [swap(pieces[j], SEQ, j) for j in range(1, seq)]

    arrived = [exchange(pack(arrays, seq, width, first, piece)) for first, piece in spans]
    core = side(GRP, 1).astype(jnp.int32).reshape(1)
    cross_grad, sums = cross_pieces(
        cross_query[0], context_key, context_value, cross_upstream[0], core, 1
    )
    key_total, value_total = reduce_text(*sums[0], core)
    grads = []
    for (first, piece), pieces in zip(spans, arrived):
        grads = unpack(exchange(self_back(pieces)), grads, full, width, first)
    query_grad, key_grad, value_grad = grads
    return query_grad[None], key_grad[None], value_grad[None], cross_grad[None], key_total, value_total


SPLIT = 3
SHARES = (8, 6)


def pair_columns(partner, base, half, offset):
    low = (lax.axis_index(SEQ) ^ partner) % 2
    return pl.multiple_of(base + low * half + offset, HD)


def pair_pack(arrays, base, half, offset, piece):
    rows = arrays[0].shape[0]
    order = (0, 3, 1, 2)

    def body(*refs):
        ins, outs = refs[:4], refs[4:8]
        held, got, sent = refs[8:]

        def fetch(half_of, i):
            columns = pl.ds(pair_columns(half_of, base, half, offset), piece)
            return pltpu.make_async_copy(ins[order[i]].at[:, columns], held.at[half_of, i], got.at[half_of, i])

        stores = [
            pltpu.make_async_copy(held.at[1, 0:2], outs[3], sent.at[3]),
            pltpu.make_async_copy(held.at[0, 0:2], outs[2], sent.at[2]),
            pltpu.make_async_copy(held.at[1], outs[1], sent.at[1]),
            pltpu.make_async_copy(held.at[0], outs[0], sent.at[0]),
        ]
        for i in range(4):
            for half_of in (1, 0):
                fetch(half_of, i).start()
        for stage in range(2):
            for half_of in (1, 0):
                for i in (2 * stage, 2 * stage + 1):
                    fetch(half_of, i).wait()
                stores[2 * stage + 1 - half_of].start()
        for store in stores:
            store.wait()

    kinds = (4, 4, 2, 2)
    return pl.pallas_call(
        body,
        out_shape=[jax.ShapeDtypeStruct((kind, rows, piece), BF16) for kind in kinds],
        in_specs=[ANY] * 4,
        out_specs=[ANY] * 4,
        scratch_shapes=[
            pltpu.VMEM((2, 4, rows, piece), BF16),
            pltpu.SemaphoreType.DMA((2, 4)),
            pltpu.SemaphoreType.DMA((4,)),
        ],
        compiler_params=pltpu.CompilerParams(vmem_limit_bytes=VMEM_LIMIT),
        cost_estimate=pl.CostEstimate(flops=0, transcendentals=0, bytes_accessed=40 * rows * piece),
    )(*arrays)


def group_of(first, heads):
    return max(g for g in range(1, 6) if heads % g == 0 and first % g == 0)


def pair_inputs(pieces, group):
    return [pl.BlockSpec(p.shape[:2] + (group * HD,), lambda h: (0, 0, h)) for p in pieces]


def pair_join(refs, at):
    own, near, far, last = refs
    queries = jnp.concatenate([ref[0, :, at] for ref in (own, near, far, last)], axis=0)
    upstream = jnp.concatenate([ref[1, :, at] for ref in (own, near, far, last)], axis=0)
    keys = jnp.concatenate([own[2, :, at], near[2, :, at]], axis=0)
    values = jnp.concatenate([own[3, :, at], near[3, :, at]], axis=0)
    return queries, keys, values, upstream


def pair_stats(pieces):
    rows, piece = pieces[0].shape[1:]
    heads = piece // HD
    group = group_of(0, heads)

    def body(*refs):
        out_ref = refs[4]
        for i in range(group):
            queries, keys, values, upstream = pair_join(refs[:4], slice(i * HD, (i + 1) * HD))
            scores = dot(keys, queries, 1, 1)
            top = jnp.max(scores, axis=0, keepdims=True)
            raw = jnp.exp2((scores - top) * (SCALE * LOG2E))
            total = jnp.sum(raw, axis=0, keepdims=True)
            grad_prob = dot(values, upstream, 1, 1)
            mean = jnp.sum(raw * grad_prob, axis=0, keepdims=True) / total
            out_ref[i, 0:1, :] = top * (SCALE * LOG2E) + jnp.log2(total)
            out_ref[i, 1:2, :] = mean

    return pl.pallas_call(
        body,
        grid=(heads // group,),
        out_shape=jax.ShapeDtypeStruct((heads, 2, 4 * rows), F32),
        in_specs=pair_inputs(pieces, group),
        out_specs=pl.BlockSpec((group, 2, 4 * rows), lambda h: (h, 0, 0)),
        compiler_params=pltpu.CompilerParams(
            vmem_limit_bytes=VMEM_LIMIT, dimension_semantics=(IN_ORDER,)
        ),
        cost_estimate=pl.CostEstimate(
            flops=32 * rows * rows * piece,
            transcendentals=8 * rows * rows * heads,
            bytes_accessed=24 * rows * piece,
        ),
    )(*pieces)


def pair_main(pieces, mine, theirs):
    rows, piece = pieces[0].shape[1:]
    heads = piece // HD
    group = group_of(0, heads)

    def body(*refs):
        mine_ref, theirs_ref, own_ref, near_ref, far_ref, last_ref = refs[4:]
        for i in range(group):
            at = slice(i * HD, (i + 1) * HD)
            queries, keys, values, upstream = pair_join(refs[:4], at)
            a, b = mine_ref[i], theirs_ref[i]
            b = jnp.concatenate([b[:, 2 * rows :], b[:, : 2 * rows]], axis=1)
            lse_a, lse_b = a[0:1], b[0:1]
            top = jnp.maximum(lse_a, lse_b)
            lse = top + jnp.log2(jnp.exp2(lse_a - top) + jnp.exp2(lse_b - top))
            delta = jnp.exp2(lse_a - lse) * a[1:2] + jnp.exp2(lse_b - lse) * b[1:2]
            scores = dot(keys, queries, 1, 1)
            weights = jnp.exp2(scores * (SCALE * LOG2E) - lse)
            grad_prob = dot(values, upstream, 1, 1)
            rounded = weights.astype(BF16)
            grad_score = (weights * (grad_prob - delta) * SCALE).astype(BF16)
            value_grad = dot(rounded, upstream, 1, 0).astype(BF16)
            key_grad = dot(grad_score, queries, 1, 0).astype(BF16)
            query_grad = dot(keys, grad_score, 0, 0).T.astype(BF16)
            for place, ref in enumerate((own_ref, near_ref)):
                part = slice(place * rows, (place + 1) * rows)
                ref[0, :, at] = query_grad[part]
                ref[1, :, at] = key_grad[part]
                ref[2, :, at] = value_grad[part]
            far_ref[:, at] = query_grad[2 * rows : 3 * rows]
            last_ref[:, at] = query_grad[3 * rows :]

    stat = pl.BlockSpec((group, 2, 4 * rows), lambda h: (h, 0, 0))
    three = pl.BlockSpec((3, rows, group * HD), lambda h: (0, 0, h))
    one = pl.BlockSpec((rows, group * HD), lambda h: (0, h))
    return pl.pallas_call(
        body,
        grid=(heads // group,),
        out_shape=[jax.ShapeDtypeStruct((3, rows, piece), BF16)] * 2
        + [jax.ShapeDtypeStruct((rows, piece), BF16)] * 2,
        in_specs=pair_inputs(pieces, group) + [stat, stat],
        out_specs=[three, three, one, one],
        compiler_params=pltpu.CompilerParams(
            vmem_limit_bytes=VMEM_LIMIT, dimension_semantics=(IN_ORDER,)
        ),
        cost_estimate=pl.CostEstimate(
            flops=80 * rows * rows * piece,
            transcendentals=8 * rows * rows * heads,
            bytes_accessed=40 * rows * piece,
        ),
    )(*pieces, mine, theirs)


def pair_unpack(own, near, far, last, before, full, base, half, offset):
    kinds, rows, piece = own.shape
    held_count = len(before)

    def body(own_ref, near_ref, far_ref, last_ref, *refs):
        outs = refs[held_count : held_count + kinds]
        held, other, total, got, sent = refs[held_count + kinds :]
        fetches = [
            pltpu.make_async_copy(own_ref, held.at[0], got.at[0]),
            pltpu.make_async_copy(far_ref, other.at[0], got.at[1]),
            pltpu.make_async_copy(near_ref, held.at[1], got.at[2]),
            pltpu.make_async_copy(last_ref, other.at[1], got.at[3]),
        ]

        def store(half_of, a):
            columns = pl.ds(pair_columns(half_of, base, half, offset), piece)
            source = total.at[half_of] if a == 0 else held.at[half_of, a]
            return pltpu.make_async_copy(source, outs[a].at[:, columns], sent.at[half_of, a])

        for fetch in fetches:
            fetch.start()
        for half_of in range(2):
            fetches[2 * half_of].wait()
            for a in range(1, kinds):
                store(half_of, a).start()
            fetches[2 * half_of + 1].wait()
            total[half_of] = (held[half_of, 0].astype(F32) + other[half_of].astype(F32)).astype(BF16)
            store(half_of, 0).start()
        for half_of in range(2):
            for a in range(kinds):
                store(half_of, a).wait()

    return pl.pallas_call(
        body,
        out_shape=[jax.ShapeDtypeStruct((rows, full), BF16)] * kinds,
        in_specs=[ANY] * (4 + held_count),
        out_specs=[ANY] * kinds,
        scratch_shapes=[
            pltpu.VMEM((2, kinds, rows, piece), BF16),
            pltpu.VMEM((2, rows, piece), BF16),
            pltpu.VMEM((2, rows, piece), BF16),
            pltpu.SemaphoreType.DMA((4,)),
            pltpu.SemaphoreType.DMA((2, kinds)),
        ],
        input_output_aliases={4 + a: a for a in range(held_count)},
        compiler_params=pltpu.CompilerParams(vmem_limit_bytes=VMEM_LIMIT),
        cost_estimate=pl.CostEstimate(flops=0, transcendentals=0, bytes_accessed=28 * rows * piece),
    )(own, near, far, last, *before)


def fold(ins, specs_in, outs, specs_out, grid, scalars, pairs):
    def body(scalar_ref, *refs):
        for i, several in enumerate(pairs):
            out = refs[len(ins) + i]
            for at, (a, b) in enumerate(several):
                total = refs[a][...].astype(F32) + refs[b][...].astype(F32)
                out[at] = total.astype(BF16).reshape(out.shape[1:])

    size = sum(2 * math.prod(o) for o in outs)
    return pl.pallas_call(
        body,
        grid_spec=pltpu.PrefetchScalarGridSpec(
            num_scalar_prefetch=1, grid=grid, in_specs=specs_in, out_specs=specs_out
        ),
        out_shape=[jax.ShapeDtypeStruct(o, BF16) for o in outs],
        compiler_params=pltpu.CompilerParams(
            vmem_limit_bytes=VMEM_LIMIT, dimension_semantics=(IN_ORDER,) * len(grid)
        ),
        cost_estimate=pl.CostEstimate(flops=size // 2, transcendentals=0, bytes_accessed=3 * size),
    )(scalars, *ins)


def reduce_text_lines(sums):
    text, columns = sums[0][0].shape
    rows, wide = text // 8, columns // 2
    place = lax.axis_index(SEQ)
    bits = jnp.stack(
        [side(GRP, 1), side(GRP, 2), side(GRP, 4), place % 2, place // 2]
    ).astype(jnp.int32)

    shape = (2, 2, 2, rows, columns)
    block = (1, 1, 1, rows, columns)

    def x_part(flip):
        return pl.BlockSpec(block, lambda i, s: (0, i, (1 - s[1]) if flip else s[1], 0, 0))

    def y_part(flip):
        return pl.BlockSpec(block, lambda i, s: (1, (1 - s[2]) if flip else s[2], i, 0, 0))

    half = pl.BlockSpec((1, rows, columns), lambda i, s: (i, 0, 0))
    specs = [x_part(True), x_part(False), y_part(True), y_part(False)]
    firsts = []
    for own, other in sums:
        received = swap(other, GRP, 1)
        a, b = own.reshape(shape), received.reshape(shape)
        x_send, x_keep, y_send, y_keep = fold(
            [a] * 4 + [b] * 4, specs * 2, [(2, rows, columns)] * 4, [half] * 4, (2,), bits,
            [[(i, 4 + i)] for i in range(4)],
        )
        x_got = swap(x_send, GRP, 2)
        y_got = swap(y_send, GRP, 4)
        firsts += [x_keep, y_keep, x_got, y_got]

    def one(bit, flip):
        return pl.BlockSpec((1, rows, wide), lambda j, s: ((1 - s[bit]) if flip else s[bit], 0, j))

    ins, specs = [], []
    for h in range(2):
        x_keep, y_keep, x_got, y_got = firsts[4 * h : 4 * h + 4]
        for flip in (True, False):
            ins += [x_keep, x_got, y_keep, y_got]
            specs += [one(2, flip), one(2, flip), one(1, flip), one(1, flip)]
    both_halves = pl.BlockSpec((2, rows, wide), lambda j, s: (0, 0, j))
    xy_send, yx_send, xy_keep, yx_keep = fold(
        ins, specs, [(2, rows, columns)] * 4, [both_halves] * 4, (2,), bits,
        [[(8 * h + 2 * i, 8 * h + 2 * i + 1) for h in range(2)] for i in range(4)],
    )
    xy_got = swap(xy_send, GRP, 4)
    yx_got = swap(yx_send, GRP, 2)

    def column(flip):
        return pl.BlockSpec((1, rows, wide), lambda j, s: (j, 0, (1 - s[3]) if flip else s[3]))

    pair = pl.BlockSpec((1, rows, wide), lambda j, s: (j, 0, 0))
    low_send0, low_send1, low_keep0, low_keep1 = fold(
        [xy_keep, yx_keep, xy_keep, yx_keep, xy_got, yx_got, xy_got, yx_got],
        [column(True), column(True), column(False), column(False)] * 2,
        [(2, rows, wide)] * 4, [pair] * 4, (2,), bits, [[(i, 4 + i)] for i in range(4)],
    )
    low_got0 = swap(low_send0, SEQ, 1)
    low_got1 = swap(low_send1, SEQ, 1)

    def high(flip):
        return pl.BlockSpec((1, rows, wide), lambda j, s: ((1 - s[4]) if flip else s[4], 0, 0))

    single = pl.BlockSpec((1, rows, wide), lambda j, s: (0, 0, 0))
    high_send0, high_send1, high_keep0, high_keep1 = fold(
        [low_keep0, low_keep1, low_keep0, low_keep1, low_got0, low_got1, low_got0, low_got1],
        [high(True), high(True), high(False), high(False)] * 2,
        [(1, rows, wide)] * 4, [single] * 4, (1,), bits, [[(i, 4 + i)] for i in range(4)],
    )
    high_got0 = swap(high_send0, SEQ, 2)
    high_got1 = swap(high_send1, SEQ, 2)
    done = fold_two(high_keep0, high_got0, high_keep1, high_got1)
    mine = [done] + [swap(done, GRP, bit) for bit in (2, 4, 6)]
    theirs = [swap(part, GRP, 1) for part in mine]
    return place_text(mine, theirs, bits)


def fold_two(a0, b0, a1, b1):
    _, rows, wide = a0.shape

    def body(a0_ref, b0_ref, a1_ref, b1_ref, out_ref):
        out_ref[0] = (a0_ref[0].astype(F32) + b0_ref[0].astype(F32)).astype(BF16)
        out_ref[1] = (a1_ref[0].astype(F32) + b1_ref[0].astype(F32)).astype(BF16)

    return pl.pallas_call(
        body,
        out_shape=jax.ShapeDtypeStruct((2, rows, wide), BF16),
        compiler_params=pltpu.CompilerParams(vmem_limit_bytes=VMEM_LIMIT),
        cost_estimate=pl.CostEstimate(flops=0, transcendentals=0, bytes_accessed=12 * rows * wide),
    )(a0, b0, a1, b1)


def place_text(mine, theirs, bits):
    ways, rows, wide = mine[0].shape
    text = ways * 4 * rows

    def body(s, *refs):
        parts, outs = refs[:8], refs[8:]
        core, x, y = s[0], s[1], s[2]
        for i in range(4):
            row = 2 * (y ^ (i // 2)) + (x ^ (i % 2))
            for way in range(ways):
                at = pl.ds(pl.multiple_of((4 * way + row) * rows, rows), rows)
                low = core == 0
                a, b = parts[i][way].astype(F32), parts[4 + i][way].astype(F32)
                outs[0][at, :] = jnp.where(low, a, b)
                outs[1][at, :] = jnp.where(low, b, a)

    col = math.gcd(wide, 640)
    part = pl.BlockSpec((ways, rows, col), lambda j, s: (0, 0, j))
    out = pl.BlockSpec((text, col), lambda j, s: (0, j))
    return pl.pallas_call(
        body,
        grid_spec=pltpu.PrefetchScalarGridSpec(
            num_scalar_prefetch=1, grid=(wide // col,), in_specs=[part] * 8, out_specs=[out] * 2
        ),
        out_shape=[jax.ShapeDtypeStruct((text, wide), F32)] * 2,
        compiler_params=pltpu.CompilerParams(
            vmem_limit_bytes=VMEM_LIMIT, dimension_semantics=(IN_ORDER,)
        ),
        cost_estimate=pl.CostEstimate(flops=0, transcendentals=0, bytes_accessed=12 * text * wide),
    )(bits, *mine, *theirs)


def pair_shards(
    self_query,
    self_key,
    self_value,
    self_upstream,
    cross_query,
    context_key,
    context_value,
    cross_upstream,
):
    full = self_query.shape[2]
    seq = lax.axis_size(SEQ)
    arrays = [self_query[0], self_key[0], self_value[0], self_upstream[0]]
    width = SPLIT * HD
    base = seq * width
    half = (full - base) // 2
    cuts = [half // HD * sum(SHARES[:c]) // sum(SHARES) * HD for c in range(len(SHARES) + 1)]
    spans = list(zip(cuts, cuts[1:]))
    held = []
    for start, stop in spans:
        own, near, far, last = pair_pack(arrays, base, half, start, stop - start)
        held.append([own] + [swap(p, SEQ, j) for j, p in ((1, near), (2, far), (3, last))])
    split = pack(arrays, seq, width, 0, width)
    split = [split[0]] + [swap(split[j], SEQ, j) for j in range(1, seq)]
    core = side(GRP, 1).astype(jnp.int32).reshape(1)
    cross_grad, sums = cross_pieces(
        cross_query[0], context_key, context_value, cross_upstream[0], core, 2
    )
    key_total, value_total = reduce_text_lines(sums)
    parts = self_back(split)
    parts = [parts[0]] + [swap(parts[j], SEQ, j) for j in range(1, seq)]
    grads = unpack(parts, [], full, width, 0)
    for c, (start, stop) in enumerate(spans):
        mine = pair_stats(held[c])
        theirs = swap(mine, SEQ, 2)
        own, near, far, last = pair_main(held[c], mine, theirs)
        near, far, last = [swap(p, SEQ, j) for j, p in ((1, near), (2, far), (3, last))]
        grads = pair_unpack(own, near, far, last, grads, full, base, half, start)
    query_grad, key_grad, value_grad = grads
    return query_grad[None], key_grad[None], value_grad[None], cross_grad[None], key_total, value_total


def solution(mesh):
    seq, grp = mesh.shape[SEQ], mesh.shape[GRP]
    pairs = seq == 4 and grp == 8

    def body(*arrays):
        return (pair_shards if pairs else split_shards)(*arrays)

    row = P(GRP, SEQ, None)
    return jax.shard_map(
        body,
        mesh=mesh,
        in_specs=(row, row, row, row, row, P(), P(), row),
        out_specs=(row, row, row, row, P(None, SEQ), P(None, SEQ)),
        check_vma=False,
    )
```

```python
import math

import jax
import jax.numpy as jnp
from jax import lax
from jax.experimental import pallas as pl
from jax.experimental.pallas import tpu as pltpu
from jax.sharding import PartitionSpec as P


HD = 128
SCALE = HD ** (-0.5)
LOG2E = math.log2(math.e)
PIECES = 2
SEQ, GRP = "seq", "grp"
IN_ORDER = "arbitrary"
F32 = jnp.float32
BF16 = jnp.bfloat16
ANY = pl.BlockSpec(memory_space=pl.ANY)
VMEM_LIMIT = 67043328


def columns_of(partner, width, first):
    owner = lax.axis_index(SEQ) ^ partner
    return pl.multiple_of(owner * width + first, HD)


def pack(arrays, count, width, first, piece):
    rows = arrays[0].shape[0]
    kinds = len(arrays)
    order = [j for j in range(count - 1, 0, -1)] + [0]

    def body(*refs):
        ins = refs[:kinds]
        outs = refs[kinds : kinds + count]
        held, got, sent = refs[kinds + count :]

        def fetch(j, a):
            return pltpu.make_async_copy(
                ins[a].at[:, pl.ds(columns_of(j, width, first), piece)], held.at[j, a], got.at[j, a]
            )

        def store(j):
            return pltpu.make_async_copy(held.at[j], outs[j], sent.at[j])

        for j in order:
            for a in range(kinds):
                fetch(j, a).start()
        for j in order:
            for a in range(kinds):
                fetch(j, a).wait()
            store(j).start()
        for j in order:
            store(j).wait()

    size = kinds * rows * piece * 2 * count
    return pl.pallas_call(
        body,
        out_shape=[jax.ShapeDtypeStruct((kinds, rows, piece), BF16)] * count,
        in_specs=[ANY] * kinds,
        out_specs=[ANY] * count,
        scratch_shapes=[
            pltpu.VMEM((count, kinds, rows, piece), BF16),
            pltpu.SemaphoreType.DMA((count, kinds)),
            pltpu.SemaphoreType.DMA((count,)),
        ],
        compiler_params=pltpu.CompilerParams(vmem_limit_bytes=VMEM_LIMIT),
        cost_estimate=pl.CostEstimate(flops=0, transcendentals=0, bytes_accessed=2 * size),
    )(*arrays)


def unpack(pieces, before, full, width, first):
    count = len(pieces)
    kinds, rows, piece = pieces[0].shape
    held_count = len(before)

    def body(*refs):
        ins = refs[:count]
        outs = refs[count + held_count : count + held_count + kinds]
        held, got, sent = refs[count + held_count + kinds :]

        def fetch(j):
            return pltpu.make_async_copy(ins[j], held.at[j], got.at[j])

        def store(j, a):
            return pltpu.make_async_copy(
                held.at[j, a], outs[a].at[:, pl.ds(columns_of(j, width, first), piece)], sent.at[j, a]
            )

        for j in range(count):
            fetch(j).start()
        for j in range(count):
            fetch(j).wait()
            for a in range(kinds):
                store(j, a).start()
        for j in range(count):
            for a in range(kinds):
                store(j, a).wait()

    size = kinds * rows * piece * 2 * count
    return pl.pallas_call(
        body,
        out_shape=[jax.ShapeDtypeStruct((rows, full), BF16)] * kinds,
        in_specs=[ANY] * (count + held_count),
        out_specs=[ANY] * kinds,
        scratch_shapes=[
            pltpu.VMEM((count, kinds, rows, piece), BF16),
            pltpu.SemaphoreType.DMA((count,)),
            pltpu.SemaphoreType.DMA((count, kinds)),
        ],
        input_output_aliases={count + a: a for a in range(held_count)},
        compiler_params=pltpu.CompilerParams(vmem_limit_bytes=VMEM_LIMIT),
        cost_estimate=pl.CostEstimate(flops=0, transcendentals=0, bytes_accessed=2 * size),
    )(*pieces, *before)


def dot(a, b, over_a, over_b):
    return lax.dot_general(a, b, (((over_a,), (over_b,)), ((), ())), preferred_element_type=F32)


def back(queries, keys, values, upstream):
    scores = dot(keys, queries, 1, 1)
    top = jnp.max(scores, axis=0, keepdims=True)
    raw = jnp.exp2((scores - top) * (SCALE * LOG2E))
    weights = raw * (1.0 / jnp.sum(raw, axis=0, keepdims=True))
    grad_prob = dot(values, upstream, 1, 1)
    rounded = weights.astype(BF16)
    delta = jnp.sum(rounded.astype(F32) * grad_prob, axis=0, keepdims=True)
    grad_score = (weights * (grad_prob - delta) * SCALE).astype(BF16)
    value_grad = dot(rounded, upstream, 1, 0)
    key_grad = dot(grad_score, queries, 1, 0)
    query_grad = dot(keys, grad_score, 0, 0).T
    return query_grad, key_grad, value_grad


def self_back(pieces):
    count = len(pieces)
    kinds, rows, piece = pieces[0].shape
    heads = piece // HD
    group = group_of(0, heads) if count * rows <= 512 else 1

    def body(*refs):
        ins, outs = refs[:count], refs[count:]
        for i in range(group):
            at = slice(i * HD, (i + 1) * HD)
            grads = back(*[jnp.concatenate([ref[a, :, at] for ref in ins], axis=0) for a in range(kinds)])
            for a in range(3):
                value = grads[a].astype(BF16)
                for j in range(count):
                    outs[j][a, :, at] = value[j * rows : (j + 1) * rows]

    tokens = count * rows
    return pl.pallas_call(
        body,
        grid=(heads // group,),
        out_shape=[jax.ShapeDtypeStruct((3, rows, piece), BF16)] * count,
        in_specs=[pl.BlockSpec((kinds, rows, group * HD), lambda h: (0, 0, h))] * count,
        out_specs=[pl.BlockSpec((3, rows, group * HD), lambda h: (0, 0, h))] * count,
        compiler_params=pltpu.CompilerParams(
            vmem_limit_bytes=VMEM_LIMIT, dimension_semantics=(IN_ORDER,)
        ),
        cost_estimate=pl.CostEstimate(
            flops=10 * tokens * tokens * piece,
            transcendentals=tokens * tokens * heads,
            bytes_accessed=7 * tokens * piece * 2,
        ),
    )(*pieces)


def cross_back(queries, keys, values, upstream, core, before, first, count):
    rows, full = queries.shape
    text = keys.shape[0]
    group = group_of(first, count)
    wide = group * HD
    start = first // group
    held = len(before)
    width = count * HD

    def body(core_ref, q_ref, k_ref, v_ref, g_ref, *refs):
        dq_ref, own_ref, other_ref = refs[held:]
        for i in range(group):
            at = slice(i * HD, (i + 1) * HD)
            query_grad, key_grad, value_grad = back(q_ref[:, at], k_ref[:, at], v_ref[:, at], g_ref[:, at])
            dq_ref[:, at] = query_grad.astype(BF16)
            low = core_ref[0] == 0
            own_ref[:, at] = jnp.where(low, key_grad, value_grad).astype(BF16)
            other_ref[:, at] = jnp.where(low, value_grad, key_grad).astype(BF16)

    small = pl.BlockSpec((rows, wide), lambda h, c: (0, start + h))
    large = pl.BlockSpec((text, wide), lambda h, c: (0, start + h))
    return pl.pallas_call(
        body,
        grid_spec=pltpu.PrefetchScalarGridSpec(
            num_scalar_prefetch=1,
            grid=(count // group,),
            in_specs=[small, large, large, small] + [ANY] * held,
            out_specs=[small] + [pl.BlockSpec((text, wide), lambda h, c: (0, h))] * 2,
        ),
        out_shape=[
            jax.ShapeDtypeStruct((rows, full), BF16),
            jax.ShapeDtypeStruct((text, width), BF16),
            jax.ShapeDtypeStruct((text, width), BF16),
        ],
        input_output_aliases={5 + i: i for i in range(held)},
        compiler_params=pltpu.CompilerParams(
            vmem_limit_bytes=VMEM_LIMIT, dimension_semantics=(IN_ORDER,)
        ),
        cost_estimate=pl.CostEstimate(
            flops=10 * rows * text * count * HD,
            transcendentals=rows * text * count,
            bytes_accessed=2 * count * HD * (3 * rows + 4 * text),
        ),
    )(core, queries, keys, values, upstream, *before)


def cross_pieces(queries, keys, values, upstream, core, pieces):
    heads = queries.shape[1] // HD
    count = heads // pieces
    grads, sums = [], []
    for i in range(pieces):
        grad, own, other = cross_back(queries, keys, values, upstream, core, grads, i * count, count)
        grads = [grad]
        sums.append((own, other))
    return grads[0], sums


def finish(own, other, core):
    rows, full = own.shape
    block = math.gcd(rows, 128)

    def body(core_ref, own_ref, other_ref, key_ref, value_ref):
        first = core_ref[0] == 0
        mine, theirs = own_ref[...].astype(F32), other_ref[...].astype(F32)
        key_ref[...] = jnp.where(first, mine, theirs)
        value_ref[...] = jnp.where(first, theirs, mine)

    spec = pl.BlockSpec((block, full), lambda i, c: (i, 0))
    return pl.pallas_call(
        body,
        grid_spec=pltpu.PrefetchScalarGridSpec(
            num_scalar_prefetch=1, grid=(rows // block,), in_specs=[spec] * 2, out_specs=[spec] * 2
        ),
        out_shape=[jax.ShapeDtypeStruct((rows, full), F32)] * 2,
        compiler_params=pltpu.CompilerParams(
            vmem_limit_bytes=VMEM_LIMIT, dimension_semantics=(IN_ORDER,)
        ),
        cost_estimate=pl.CostEstimate(flops=0, transcendentals=0, bytes_accessed=12 * rows * full),
    )(core, own, other)


def swap(value, axis, bit):
    size = lax.axis_size(axis)
    return lax.ppermute(value, axis, [(i, i ^ bit) for i in range(size)])


def side(axis, bit):
    return (lax.axis_index(axis) // bit) % 2


def pick(value, index, dim):
    return lax.dynamic_index_in_dim(value, index, dim, keepdims=False)


def add(a, b):
    return (a.astype(F32) + b.astype(F32)).astype(BF16)


def halve(value, dim, axis, bit):
    mine = side(axis, bit)
    return add(pick(value, mine, dim), swap(pick(value, 1 - mine, dim), axis, bit))


def both(value, other, axis, bit, dim):
    low = side(axis, bit) == 0
    return jnp.stack([jnp.where(low, value, other), jnp.where(low, other, value)], axis=dim)


def reduce_text(own, other, core):
    grp, seq = lax.axis_size(GRP), lax.axis_size(SEQ)
    bits = [1 << i for i in range(1, grp.bit_length() - 1)]
    seq_bits = [1 << i for i in range(seq.bit_length() - 1)]
    text, full = own.shape
    total = add(own, swap(other, GRP, 1))
    ways = 2
    split = total.reshape((ways,) + (2,) * len(bits) + (text // (ways * grp // 2), full))
    parts = []
    for way in range(ways):
        part = split[way]
        names = list(bits)
        for bit in bits[way:] + bits[:way]:
            part = halve(part, names.index(bit), GRP, bit)
            names.remove(bit)
        parts.append(part)
    part = jnp.stack(parts)
    part = part.reshape(part.shape[:2] + (2,) * len(seq_bits) + (full // seq,))
    left = list(reversed(seq_bits))
    for bit in seq_bits:
        part = halve(part, 2 + left.index(bit), SEQ, bit)
        left.remove(bit)
    for bit in reversed(bits):
        part = both(part, swap(part, GRP, bit), GRP, bit, 1)
    shape = (text, full // seq)
    return finish(part.reshape(shape), swap(part, GRP, 1).reshape(shape), core)


def split_shards(
    self_query,
    self_key,
    self_value,
    self_upstream,
    cross_query,
    context_key,
    context_value,
    cross_upstream,
):
    full = self_query.shape[2]
    seq = lax.axis_size(SEQ)
    width = full // seq
    heads = width // HD
    cuts = [heads * i // PIECES for i in range(PIECES + 1)]
    spans = [(a * HD, (b - a) * HD) for a, b in zip(cuts, cuts[1:]) if b > a]
    arrays = [self_query[0], self_key[0], self_value[0], self_upstream[0]]

    def exchange(pieces):
        return [pieces[0]] + [swap(pieces[j], SEQ, j) for j in range(1, seq)]

    arrived = [exchange(pack(arrays, seq, width, first, piece)) for first, piece in spans]
    core = side(GRP, 1).astype(jnp.int32).reshape(1)
    cross_grad, sums = cross_pieces(
        cross_query[0], context_key, context_value, cross_upstream[0], core, 1
    )
    key_total, value_total = reduce_text(*sums[0], core)
    grads = []
    for (first, piece), pieces in zip(spans, arrived):
        grads = unpack(exchange(self_back(pieces)), grads, full, width, first)
    query_grad, key_grad, value_grad = grads
    return query_grad[None], key_grad[None], value_grad[None], cross_grad[None], key_total, value_total


SPLIT = 3
SHARES = (8, 6)


def pair_columns(partner, base, half, offset):
    low = (lax.axis_index(SEQ) ^ partner) % 2
    return pl.multiple_of(base + low * half + offset, HD)


def pair_pack(arrays, base, half, offset, piece):
    rows = arrays[0].shape[0]
    order = (0, 3, 1, 2)

    def body(*refs):
        ins, outs = refs[:4], refs[4:8]
        held, got, sent = refs[8:]

        def fetch(half_of, i):
            columns = pl.ds(pair_columns(half_of, base, half, offset), piece)
            return pltpu.make_async_copy(ins[order[i]].at[:, columns], held.at[half_of, i], got.at[half_of, i])

        stores = [
            pltpu.make_async_copy(held.at[1, 0:2], outs[3], sent.at[3]),
            pltpu.make_async_copy(held.at[0, 0:2], outs[2], sent.at[2]),
            pltpu.make_async_copy(held.at[1], outs[1], sent.at[1]),
            pltpu.make_async_copy(held.at[0], outs[0], sent.at[0]),
        ]
        for i in range(4):
            for half_of in (1, 0):
                fetch(half_of, i).start()
        for stage in range(2):
            for half_of in (1, 0):
                for i in (2 * stage, 2 * stage + 1):
                    fetch(half_of, i).wait()
                stores[2 * stage + 1 - half_of].start()
        for store in stores:
            store.wait()

    kinds = (4, 4, 2, 2)
    return pl.pallas_call(
        body,
        out_shape=[jax.ShapeDtypeStruct((kind, rows, piece), BF16) for kind in kinds],
        in_specs=[ANY] * 4,
        out_specs=[ANY] * 4,
        scratch_shapes=[
            pltpu.VMEM((2, 4, rows, piece), BF16),
            pltpu.SemaphoreType.DMA((2, 4)),
            pltpu.SemaphoreType.DMA((4,)),
        ],
        compiler_params=pltpu.CompilerParams(vmem_limit_bytes=VMEM_LIMIT),
        cost_estimate=pl.CostEstimate(flops=0, transcendentals=0, bytes_accessed=40 * rows * piece),
    )(*arrays)


def group_of(first, heads):
    return max(g for g in range(1, 6) if heads % g == 0 and first % g == 0)


def pair_inputs(pieces, group):
    return [pl.BlockSpec(p.shape[:2] + (group * HD,), lambda h: (0, 0, h)) for p in pieces]


def pair_join(refs, at):
    own, near, far, last = refs
    queries = jnp.concatenate([ref[0, :, at] for ref in (own, near, far, last)], axis=0)
    upstream = jnp.concatenate([ref[1, :, at] for ref in (own, near, far, last)], axis=0)
    keys = jnp.concatenate([own[2, :, at], near[2, :, at]], axis=0)
    values = jnp.concatenate([own[3, :, at], near[3, :, at]], axis=0)
    return queries, keys, values, upstream


def pair_stats(pieces):
    rows, piece = pieces[0].shape[1:]
    heads = piece // HD
    group = group_of(0, heads)

    def body(*refs):
        out_ref = refs[4]
        for i in range(group):
            queries, keys, values, upstream = pair_join(refs[:4], slice(i * HD, (i + 1) * HD))
            scores = dot(keys, queries, 1, 1)
            top = jnp.max(scores, axis=0, keepdims=True)
            raw = jnp.exp2((scores - top) * (SCALE * LOG2E))
            total = jnp.sum(raw, axis=0, keepdims=True)
            grad_prob = dot(values, upstream, 1, 1)
            mean = jnp.sum(raw * grad_prob, axis=0, keepdims=True) / total
            out_ref[i, 0:1, :] = top * (SCALE * LOG2E) + jnp.log2(total)
            out_ref[i, 1:2, :] = mean

    return pl.pallas_call(
        body,
        grid=(heads // group,),
        out_shape=jax.ShapeDtypeStruct((heads, 2, 4 * rows), F32),
        in_specs=pair_inputs(pieces, group),
        out_specs=pl.BlockSpec((group, 2, 4 * rows), lambda h: (h, 0, 0)),
        compiler_params=pltpu.CompilerParams(
            vmem_limit_bytes=VMEM_LIMIT, dimension_semantics=(IN_ORDER,)
        ),
        cost_estimate=pl.CostEstimate(
            flops=32 * rows * rows * piece,
            transcendentals=8 * rows * rows * heads,
            bytes_accessed=24 * rows * piece,
        ),
    )(*pieces)


def pair_main(pieces, mine, theirs):
    rows, piece = pieces[0].shape[1:]
    heads = piece // HD
    group = group_of(0, heads)

    def body(*refs):
        mine_ref, theirs_ref, own_ref, near_ref, far_ref, last_ref = refs[4:]
        for i in range(group):
            at = slice(i * HD, (i + 1) * HD)
            queries, keys, values, upstream = pair_join(refs[:4], at)
            a, b = mine_ref[i], theirs_ref[i]
            b = jnp.concatenate([b[:, 2 * rows :], b[:, : 2 * rows]], axis=1)
            lse_a, lse_b = a[0:1], b[0:1]
            top = jnp.maximum(lse_a, lse_b)
            lse = top + jnp.log2(jnp.exp2(lse_a - top) + jnp.exp2(lse_b - top))
            delta = jnp.exp2(lse_a - lse) * a[1:2] + jnp.exp2(lse_b - lse) * b[1:2]
            scores = dot(keys, queries, 1, 1)
            weights = jnp.exp2(scores * (SCALE * LOG2E) - lse)
            grad_prob = dot(values, upstream, 1, 1)
            rounded = weights.astype(BF16)
            grad_score = (weights * (grad_prob - delta) * SCALE).astype(BF16)
            value_grad = dot(rounded, upstream, 1, 0).astype(BF16)
            key_grad = dot(grad_score, queries, 1, 0).astype(BF16)
            query_grad = dot(keys, grad_score, 0, 0).T.astype(BF16)
            for place, ref in enumerate((own_ref, near_ref)):
                part = slice(place * rows, (place + 1) * rows)
                ref[0, :, at] = query_grad[part]
                ref[1, :, at] = key_grad[part]
                ref[2, :, at] = value_grad[part]
            far_ref[:, at] = query_grad[2 * rows : 3 * rows]
            last_ref[:, at] = query_grad[3 * rows :]

    stat = pl.BlockSpec((group, 2, 4 * rows), lambda h: (h, 0, 0))
    three = pl.BlockSpec((3, rows, group * HD), lambda h: (0, 0, h))
    one = pl.BlockSpec((rows, group * HD), lambda h: (0, h))
    return pl.pallas_call(
        body,
        grid=(heads // group,),
        out_shape=[jax.ShapeDtypeStruct((3, rows, piece), BF16)] * 2
        + [jax.ShapeDtypeStruct((rows, piece), BF16)] * 2,
        in_specs=pair_inputs(pieces, group) + [stat, stat],
        out_specs=[three, three, one, one],
        compiler_params=pltpu.CompilerParams(
            vmem_limit_bytes=VMEM_LIMIT, dimension_semantics=(IN_ORDER,)
        ),
        cost_estimate=pl.CostEstimate(
            flops=80 * rows * rows * piece,
            transcendentals=8 * rows * rows * heads,
            bytes_accessed=40 * rows * piece,
        ),
    )(*pieces, mine, theirs)


def pair_unpack(parts, before, full, base, half, offset):
    count = len(parts)
    kinds, rows, piece = parts[0][1].shape
    held_count = len(before)

    def body(*refs):
        ins = refs[: 2 * count]
        outs = refs[2 * count + held_count : 2 * count + held_count + kinds]
        held, other, total, got, sent = refs[2 * count + held_count + kinds :]
        fetches = []
        for i in range(count):
            fetches.append(pltpu.make_async_copy(ins[2 * i], held.at[i], got.at[2 * i]))
            fetches.append(pltpu.make_async_copy(ins[2 * i + 1], other.at[i], got.at[2 * i + 1]))

        def store(i, a):
            columns = pl.ds(pair_columns(parts[i][0], base, half, offset), piece)
            source = total.at[i] if a == 0 else held.at[i, a]
            return pltpu.make_async_copy(source, outs[a].at[:, columns], sent.at[i, a])

        for fetch in fetches:
            fetch.start()
        for i in range(count):
            fetches[2 * i].wait()
            for a in range(1, kinds):
                store(i, a).start()
            fetches[2 * i + 1].wait()
            total[i] = (held[i, 0].astype(F32) + other[i].astype(F32)).astype(BF16)
            store(i, 0).start()
        for i in range(count):
            for a in range(kinds):
                store(i, a).wait()

    return pl.pallas_call(
        body,
        out_shape=[jax.ShapeDtypeStruct((rows, full), BF16)] * kinds,
        in_specs=[ANY] * (2 * count + held_count),
        out_specs=[ANY] * kinds,
        scratch_shapes=[
            pltpu.VMEM((count, kinds, rows, piece), BF16),
            pltpu.VMEM((count, rows, piece), BF16),
            pltpu.VMEM((count, rows, piece), BF16),
            pltpu.SemaphoreType.DMA((2 * count,)),
            pltpu.SemaphoreType.DMA((count, kinds)),
        ],
        input_output_aliases={2 * count + a: a for a in range(held_count)},
        compiler_params=pltpu.CompilerParams(vmem_limit_bytes=VMEM_LIMIT),
        cost_estimate=pl.CostEstimate(flops=0, transcendentals=0, bytes_accessed=14 * count * rows * piece),
    )(*[array for _, *arrays in parts for array in arrays], *before)


def fold(ins, specs_in, outs, specs_out, grid, scalars, pairs):
    def body(scalar_ref, *refs):
        for i, several in enumerate(pairs):
            out = refs[len(ins) + i]
            for at, (a, b) in enumerate(several):
                total = refs[a][...].astype(F32) + refs[b][...].astype(F32)
                out[at] = total.astype(BF16).reshape(out.shape[1:])

    size = sum(2 * math.prod(o) for o in outs)
    return pl.pallas_call(
        body,
        grid_spec=pltpu.PrefetchScalarGridSpec(
            num_scalar_prefetch=1, grid=grid, in_specs=specs_in, out_specs=specs_out
        ),
        out_shape=[jax.ShapeDtypeStruct(o, BF16) for o in outs],
        compiler_params=pltpu.CompilerParams(
            vmem_limit_bytes=VMEM_LIMIT, dimension_semantics=(IN_ORDER,) * len(grid)
        ),
        cost_estimate=pl.CostEstimate(flops=size // 2, transcendentals=0, bytes_accessed=3 * size),
    )(scalars, *ins)


def reduce_text_lines(sums):
    text, columns = sums[0][0].shape
    rows, wide = text // 8, columns // 2
    place = lax.axis_index(SEQ)
    bits = jnp.stack(
        [side(GRP, 1), side(GRP, 2), side(GRP, 4), place % 2, place // 2]
    ).astype(jnp.int32)

    shape = (2, 2, 2, rows, columns)
    block = (1, 1, 1, rows, columns)

    def x_part(flip):
        return pl.BlockSpec(block, lambda i, s: (0, i, (1 - s[1]) if flip else s[1], 0, 0))

    def y_part(flip):
        return pl.BlockSpec(block, lambda i, s: (1, (1 - s[2]) if flip else s[2], i, 0, 0))

    half = pl.BlockSpec((1, rows, columns), lambda i, s: (i, 0, 0))
    specs = [x_part(True), x_part(False), y_part(True), y_part(False)]
    firsts = []
    for own, other in sums:
        received = swap(other, GRP, 1)
        a, b = own.reshape(shape), received.reshape(shape)
        x_send, x_keep, y_send, y_keep = fold(
            [a] * 4 + [b] * 4, specs * 2, [(2, rows, columns)] * 4, [half] * 4, (2,), bits,
            [[(i, 4 + i)] for i in range(4)],
        )
        x_got = swap(x_send, GRP, 2)
        y_got = swap(y_send, GRP, 4)
        firsts += [x_keep, y_keep, x_got, y_got]

    def one(bit, flip):
        return pl.BlockSpec((1, rows, wide), lambda j, s: ((1 - s[bit]) if flip else s[bit], 0, j))

    ins, specs = [], []
    for h in range(2):
        x_keep, y_keep, x_got, y_got = firsts[4 * h : 4 * h + 4]
        for flip in (True, False):
            ins += [x_keep, x_got, y_keep, y_got]
            specs += [one(2, flip), one(2, flip), one(1, flip), one(1, flip)]
    both_halves = pl.BlockSpec((2, rows, wide), lambda j, s: (0, 0, j))
    xy_send, yx_send, xy_keep, yx_keep = fold(
        ins, specs, [(2, rows, columns)] * 4, [both_halves] * 4, (2,), bits,
        [[(8 * h + 2 * i, 8 * h + 2 * i + 1) for h in range(2)] for i in range(4)],
    )
    xy_got = swap(xy_send, GRP, 4)
    yx_got = swap(yx_send, GRP, 2)

    def column(flip):
        return pl.BlockSpec((1, rows, wide), lambda j, s: (j, 0, (1 - s[3]) if flip else s[3]))

    pair = pl.BlockSpec((1, rows, wide), lambda j, s: (j, 0, 0))
    low_send0, low_send1, low_keep0, low_keep1 = fold(
        [xy_keep, yx_keep, xy_keep, yx_keep, xy_got, yx_got, xy_got, yx_got],
        [column(True), column(True), column(False), column(False)] * 2,
        [(2, rows, wide)] * 4, [pair] * 4, (2,), bits, [[(i, 4 + i)] for i in range(4)],
    )
    low_got0 = swap(low_send0, SEQ, 1)
    low_got1 = swap(low_send1, SEQ, 1)

    def high(flip):
        return pl.BlockSpec((1, rows, wide), lambda j, s: ((1 - s[4]) if flip else s[4], 0, 0))

    single = pl.BlockSpec((1, rows, wide), lambda j, s: (0, 0, 0))
    high_send0, high_send1, high_keep0, high_keep1 = fold(
        [low_keep0, low_keep1, low_keep0, low_keep1, low_got0, low_got1, low_got0, low_got1],
        [high(True), high(True), high(False), high(False)] * 2,
        [(1, rows, wide)] * 4, [single] * 4, (1,), bits, [[(i, 4 + i)] for i in range(4)],
    )
    high_got0 = swap(high_send0, SEQ, 2)
    high_got1 = swap(high_send1, SEQ, 2)
    done = fold_two(high_keep0, high_got0, high_keep1, high_got1)
    mine = [done] + [swap(done, GRP, bit) for bit in (2, 4, 6)]
    theirs = [swap(part, GRP, 1) for part in mine]
    return place_text(mine, theirs, bits)


def fold_two(a0, b0, a1, b1):
    _, rows, wide = a0.shape

    def body(a0_ref, b0_ref, a1_ref, b1_ref, out_ref):
        out_ref[0] = (a0_ref[0].astype(F32) + b0_ref[0].astype(F32)).astype(BF16)
        out_ref[1] = (a1_ref[0].astype(F32) + b1_ref[0].astype(F32)).astype(BF16)

    return pl.pallas_call(
        body,
        out_shape=jax.ShapeDtypeStruct((2, rows, wide), BF16),
        compiler_params=pltpu.CompilerParams(vmem_limit_bytes=VMEM_LIMIT),
        cost_estimate=pl.CostEstimate(flops=0, transcendentals=0, bytes_accessed=12 * rows * wide),
    )(a0, b0, a1, b1)


def place_text(mine, theirs, bits):
    ways, rows, wide = mine[0].shape
    text = ways * 4 * rows

    def body(s, *refs):
        parts, outs = refs[:8], refs[8:]
        core, x, y = s[0], s[1], s[2]
        for i in range(4):
            row = 2 * (y ^ (i // 2)) + (x ^ (i % 2))
            for way in range(ways):
                at = pl.ds(pl.multiple_of((4 * way + row) * rows, rows), rows)
                low = core == 0
                a, b = parts[i][way].astype(F32), parts[4 + i][way].astype(F32)
                outs[0][at, :] = jnp.where(low, a, b)
                outs[1][at, :] = jnp.where(low, b, a)

    col = math.gcd(wide, 640)
    part = pl.BlockSpec((ways, rows, col), lambda j, s: (0, 0, j))
    out = pl.BlockSpec((text, col), lambda j, s: (0, j))
    return pl.pallas_call(
        body,
        grid_spec=pltpu.PrefetchScalarGridSpec(
            num_scalar_prefetch=1, grid=(wide // col,), in_specs=[part] * 8, out_specs=[out] * 2
        ),
        out_shape=[jax.ShapeDtypeStruct((text, wide), F32)] * 2,
        compiler_params=pltpu.CompilerParams(
            vmem_limit_bytes=VMEM_LIMIT, dimension_semantics=(IN_ORDER,)
        ),
        cost_estimate=pl.CostEstimate(flops=0, transcendentals=0, bytes_accessed=12 * text * wide),
    )(bits, *mine, *theirs)


def pair_shards(
    self_query,
    self_key,
    self_value,
    self_upstream,
    cross_query,
    context_key,
    context_value,
    cross_upstream,
):
    full = self_query.shape[2]
    seq = lax.axis_size(SEQ)
    arrays = [self_query[0], self_key[0], self_value[0], self_upstream[0]]
    width = SPLIT * HD
    base = seq * width
    half = (full - base) // 2
    cuts = [half // HD * sum(SHARES[:c]) // sum(SHARES) * HD for c in range(len(SHARES) + 1)]
    spans = list(zip(cuts, cuts[1:]))
    held = []
    for start, stop in spans:
        own, near, far, last = pair_pack(arrays, base, half, start, stop - start)
        held.append([own] + [swap(p, SEQ, j) for j, p in ((1, near), (2, far), (3, last))])
    split = pack(arrays, seq, width, 0, width)
    split = [split[0]] + [swap(split[j], SEQ, j) for j in range(1, seq)]
    core = side(GRP, 1).astype(jnp.int32).reshape(1)
    cross_grad, sums = cross_pieces(
        cross_query[0], context_key, context_value, cross_upstream[0], core, 2
    )
    key_total, value_total = reduce_text_lines(sums)
    parts = self_back(split)
    parts = [parts[0]] + [swap(parts[j], SEQ, j) for j in range(1, seq)]
    grads = unpack(parts, [], full, width, 0)
    for c, (start, stop) in enumerate(spans):
        mine = pair_stats(held[c])
        theirs = swap(mine, SEQ, 2)
        own, near, far, last = pair_main(held[c], mine, theirs)
        near, far, last = [swap(p, SEQ, j) for j, p in ((1, near), (2, far), (3, last))]
        parts = [(0, own, far), (1, near, last)]
        for some in [parts] if c + 1 < len(spans) else [parts[:1], parts[1:]]:
            grads = pair_unpack(some, grads, full, base, half, start)
    query_grad, key_grad, value_grad = grads
    return query_grad[None], key_grad[None], value_grad[None], cross_grad[None], key_total, value_total


def solution(mesh):
    seq, grp = mesh.shape[SEQ], mesh.shape[GRP]
    pairs = seq == 4 and grp == 8

    def body(*arrays):
        return (pair_shards if pairs else split_shards)(*arrays)

    row = P(GRP, SEQ, None)
    return jax.shard_map(
        body,
        mesh=mesh,
        in_specs=(row, row, row, row, row, P(), P(), row),
        out_specs=(row, row, row, row, P(None, SEQ), P(None, SEQ)),
        check_vma=False,
    )
```
